32 devices in a mesh: axial: 8 (over y, x, core), span: 4 (over z).
Axes of the slice: x: 2, y: 2, z: 4, core: 2. Of those that a mesh axis runs over, the one named last changes fastest.
Arguments:
- stiffness: float32 [64, 32, 128], P('axial', 'span'), may hold values from 0.2 to 5
- adjoint_rhs: float32 [3, 64, 32, 128], P(None, 'axial', 'span'), may hold values from -96 to 96
- surf_cell: int32 [8, 2048], P('axial', 'span'), may hold values from 0 to 8191
- surf_live: int32 [8, 2048], P('axial', 'span'), may hold values from 0 to 1, as said below
- ffd_index: int32 [8, 8, 2048], P(None, 'axial', 'span'), may hold values from 0 to 4095, as said below
- ffd_weight: float32 [8, 8, 2048], P(None, 'axial', 'span'), may hold values from 0.03 to 0.3
- surf_direct: float32 [3, 8, 2048], P(None, 'axial', 'span'), may hold values from -6 to 6
- surf_metric: float32 [3, 8, 2048], P(None, 'axial', 'span'), may hold values from -6 to 6
Outputs:
- adjoint: float32 [3, 64, 32, 128], P(None, 'axial', 'span')
- ffd_grad: float32 [4096, 3], P(('axial', 'span'))
The draws below stay inside these ranges and needn't reach their ends.
Inputs may be any that keep to these rules, and one draw needn't show every extreme that they name: `surf_live`: some device has all 512 of its slots live in every draw; the share of live slots differs from device to device. `ffd_index`: for the device at axial index u and span index t, with f = u times the span axis's size plus t and P = f plus half the number of devices, every control point named by its slots is (f - 1) * 128 + r or (P - 1) * 128 + r modulo 4096, for some r from 0 to 383.
All inputs are finite; a program needn't handle non-finite values.
Results may differ from the reference program's by a relative error of at most 0.000076.
Values sent between devices are 32-bit elements; how exact they have to be, the bound alone decides.
A program may use at most 64 MiB of HBM per device.

```python
import math
import jax
import jax.numpy as jnp

CX = 8
CY = 8
CZ = 128
SWEEPS = 3
NFFD = 4096
NEAR = 8
SLOTS = 512
NX = 64
NY = 32
N_AXIAL = 8
N_SPAN = 4


def draw_surf_live(key, part):
    level_key = jax.random.fold_in(key, 11)
    chosen_key = jax.random.fold_in(key, 12)
    rolls_key = jax.random.fold_in(key, 13)
    device_count = N_AXIAL * N_SPAN
    levels = jax.random.randint(level_key, (device_count,), 1, 9)
    chosen = jax.random.randint(chosen_key, (), 0, device_count)
    levels = jnp.where(jnp.arange(device_count) == chosen, 8, levels)
    rolls = jax.random.randint(rolls_key, (device_count, SLOTS), 0, 8)
    live_mask = (rolls < levels[:, None]).astype(jnp.int32)
    return live_mask.reshape(N_AXIAL, N_SPAN * SLOTS)


def draw_ffd_index(key, part):
    index_key = jax.random.fold_in(key, 21)
    device_count = N_AXIAL * N_SPAN
    owned = NFFD // device_count
    flat_device = jnp.arange(N_AXIAL, dtype=jnp.int32)[:, None] * N_SPAN + jnp.arange(N_SPAN * SLOTS, dtype=jnp.int32)[None, :] // SLOTS
    shifts = jax.random.randint(index_key, (NEAR, N_AXIAL, N_SPAN * SLOTS), 0, 6 * owned)
    own_base = (flat_device * owned - owned)[None]
    paired_base = ((flat_device + device_count // 2) * owned - owned)[None]
    chosen = jnp.where(shifts < 3 * owned, own_base + shifts, paired_base + shifts - 3 * owned)
    return chosen % NFFD


def plant(values, rng, low, top_value):
    extent = values.shape
    spot = [jax.random.randint(jax.random.fold_in(rng, axis), (), 0, extent[axis]) for axis in range(len(extent))]
    values = values.at[tuple(spot)].set(low)
    longest = extent.index(max(extent))
    spot[longest] = (spot[longest] + 1) % extent[longest]
    return values.at[tuple(spot)].set(top_value)


def block_scale(stream_key, extent, pieces, low, top_value):
    loudness, own = 1.0, jax.random.fold_in(stream_key, 6)
    for dim, parts in pieces:
        draws = jnp.exp(jax.random.uniform(jax.random.fold_in(own, dim), (parts,), jnp.float32, low / len(pieces), top_value / len(pieces)))
        loudness = loudness * jnp.repeat(draws, extent[dim] // parts).reshape([-1 if axis == dim else 1 for axis in range(len(extent))])
    return loudness


def normal_values(stream_key, shape, deviation, most, pieces=(), held_as=jnp.bfloat16):
    entries = jax.random.normal(stream_key, shape, jnp.float32) * deviation
    if len(pieces) > 0:
        entries = block_scale(stream_key, shape, pieces, -0.22, 0.18) * entries
    return jnp.clip(entries, min=-most, max=most).astype(held_as)


def setup_inputs(seed: int = 0) -> dict:
    key_list = jax.random.split(jax.random.key(seed), 9)
    return {
        "stiffness": jnp.clip(jnp.exp(math.log(5.0) - 3.218876 * jax.random.uniform(key_list[0], (NX, NY, CZ), jnp.float32) ** block_scale(key_list[0], (NX, NY, CZ), ((0, 8), (1, 4)), -0.2, 0.2)), 0.2, 5.0),
        "adjoint_rhs": normal_values(key_list[1], (3, NX, NY, CZ), 16.0, 96.0, ((1, 8), (2, 4)), jnp.float32),
        "surf_cell": plant(jax.random.randint(key_list[2], (N_AXIAL, N_SPAN * SLOTS), 0, CX * CY * CZ), jax.random.fold_in(key_list[2], 1), 0, (CX * CY * CZ) - 1).astype(jnp.int32),
        "surf_live": draw_surf_live(jax.random.fold_in(key_list[8], 71), 0),
        "ffd_index": draw_ffd_index(jax.random.fold_in(key_list[8], 71), 0),
        "ffd_weight": jnp.clip(jnp.exp(math.log(0.3) - 2.3025852 * jax.random.uniform(key_list[5], (NEAR, N_AXIAL, N_SPAN * SLOTS), jnp.float32) ** block_scale(key_list[5], (NEAR, N_AXIAL, N_SPAN * SLOTS), ((1, 8), (2, 4)), -0.2, 0.2)), 0.03, 0.3),
        "surf_direct": normal_values(key_list[6], (3, N_AXIAL, N_SPAN * SLOTS), 1.0, 6.0, ((1, 8), (2, 4)), jnp.float32),
        "surf_metric": normal_values(key_list[7], (3, N_AXIAL, N_SPAN * SLOTS), 1.0, 6.0, ((1, 8), (2, 4)), jnp.float32),
    }


neighbor_offsets = [(step_x, step_y, step_z) for step_x in (-1, 0, 1) for step_y in (-1, 0, 1) for step_z in (-1, 0, 1) if (step_x, step_y, step_z) != (0, 0, 0)]


def weight_of(offset):
    distance = abs(offset[0]) + abs(offset[1]) + abs(offset[2])
    return {1: 1.0, 2: 0.5, 3: 0.25}[distance], distance


def neighbor(values, step_x, step_y, step_z):
    row_count = values.shape[-3] - 2
    col_count = values.shape[-2] - 2
    window = values[..., 1 + step_x:1 + step_x + row_count, 1 + step_y:1 + step_y + col_count, :]
    if step_z != 0:
        window = jnp.roll(window, -step_z, axis=-1)
    return window


def diagonal_of(stiff_pad):
    summed = None
    for offset in neighbor_offsets:
        weight, distance = weight_of(offset)
        factor = 1.25 * weight + (0.25 if distance == 2 else 0.0)
        contribution = factor * neighbor(stiff_pad, *offset)
        summed = contribution if summed is None else summed + contribution
    return summed


def apply_operator(adjoint_pad, stiff_pad, diagonal):
    center = adjoint_pad[:, 1:-1, 1:-1, :]
    result = [diagonal * center[0], diagonal * center[1], diagonal * center[2]]
    for offset in neighbor_offsets:
        weight, distance = weight_of(offset)
        weighted = neighbor(stiff_pad, *offset)[None] * neighbor(adjoint_pad, *offset)
        for component in range(3):
            result[component] = result[component] - weight * weighted[component]
        if distance == 2:
            dims = [axis_pos for axis_pos in range(3) if offset[axis_pos] != 0]
            first_dim, second_dim = dims[0], dims[1]
            parity = 0.25 * offset[first_dim] * offset[second_dim]
            result[first_dim] = result[first_dim] - parity * weighted[second_dim]
            result[second_dim] = result[second_dim] - parity * weighted[first_dim]
    return jnp.stack(result)


def reference(stiffness, adjoint_rhs, surf_cell, surf_live, ffd_index, ffd_weight, surf_direct, surf_metric):
    stiff_pad = jnp.pad(stiffness, ((1, 1), (1, 1), (0, 0)))
    diagonal = diagonal_of(stiff_pad)
    adjoint = adjoint_rhs / diagonal
    for iteration in range(SWEEPS):
        adjoint_pad = jnp.pad(adjoint, ((0, 0), (1, 1), (1, 1), (0, 0)))
        adjoint = adjoint + (adjoint_rhs - apply_operator(adjoint_pad, stiff_pad, diagonal)) / diagonal
    span_block = jnp.arange(N_SPAN * SLOTS, dtype=jnp.int32) // SLOTS
    global_x = jnp.arange(N_AXIAL, dtype=jnp.int32)[:, None] * CX + surf_cell // (CY * CZ)
    global_y = span_block[None, :] * CY + (surf_cell // CZ) % CY
    global_z = surf_cell % CZ
    adjoint_at = adjoint[:, global_x, global_y, global_z]
    sensitivity = surf_live.astype(jnp.float32) * (surf_direct - surf_metric * adjoint_at)
    contribution = ffd_weight[:, None] * sensitivity[None]
    flat_terms = jnp.transpose(contribution, (0, 2, 3, 1)).reshape(-1, 3)
    ffd_grad = jax.ops.segment_sum(flat_terms, ffd_index.reshape(-1), num_segments=NFFD)
    return adjoint, ffd_grad
```

```python
import functools

import jax
import jax.numpy as jnp
from jax import lax
from jax.experimental import pallas as pl
from jax.experimental.pallas import tpu as pltpu
from jax.sharding import PartitionSpec as P

SWEEPS = 3
NFFD = 4096
CHUNK = 2
MESH = pl.DeviceIdType.MESH
DIRS = [(dx, dy) for dx in (-1, 0, 1) for dy in (-1, 0, 1) if (dx, dy) != (0, 0)]


def yshift(a, step):
    return pltpu.roll(a, (-step) % 16, 1)


def zshift(a, step):
    return pltpu.roll(a, (-step) % 128, 2)


def chunks(lo, hi):
    return [(c, min(CHUNK, hi - c)) for c in range(lo, hi, CHUNK)]


def kernel(
    n_axial, n_span,
    stiff, rhs, cell, live, index, weight, direct, metric,
    adj_out, grad_out,
    s_ext, r_ext, inv_ref, v_ref, p_ref, q_ref, own_v,
    cell_v, live_v, index_v, weight_v, direct_v, metric_v,
    zhot, lohot, mw, send_g, recv_g, grad_v,
    halo_send, halo_recv, g_send, g_recv, local_sem,
):
    u = lax.axis_index("axial")
    t = lax.axis_index("span")
    count = n_axial * n_span
    owned = NFFD // count
    f = u * n_span + t
    lows = lohot.shape[1]

    loads = [
        pltpu.make_async_copy(stiff, s_ext.at[pl.ds(4, 8), pl.ds(0, 8)], local_sem.at[0]),
        pltpu.make_async_copy(rhs, r_ext.at[:, pl.ds(4, 8), pl.ds(0, 8)], local_sem.at[1]),
        pltpu.make_async_copy(cell, cell_v, local_sem.at[2]),
        pltpu.make_async_copy(live, live_v, local_sem.at[3]),
        pltpu.make_async_copy(index, index_v, local_sem.at[4]),
        pltpu.make_async_copy(weight, weight_v, local_sem.at[5]),
        pltpu.make_async_copy(direct, direct_v, local_sem.at[6]),
        pltpu.make_async_copy(metric, metric_v, local_sem.at[7]),
    ]
    for load in loads[2:]:
        load.start()

    zero = jnp.zeros((8, 8, 128), jnp.float32)
    zero4 = jnp.zeros((4, 16, 128), jnp.float32)
    s_ext[0:4] = zero4
    s_ext[12:16] = zero4
    s_ext[4:12, 8:16] = zero
    for i in range(3):
        r_ext[i, 0:4] = zero4
        r_ext[i, 12:16] = zero4
        r_ext[i, 4:12, 8:16] = zero
    loads[0].start()
    loads[1].start()

    def owner(h):
        base = f + (count - 1) + h if h < 3 else f + (count - 1) + count // 2 + (h - 3)
        d = lax.rem(base, count)
        return (lax.div(d, n_span), lax.rem(d, n_span))

    def sender(h):
        base = f + count + 1 - h if h < 3 else f + count // 2 + count + 1 - (h - 3)
        d = lax.rem(base, count)
        return (lax.div(d, n_span), lax.rem(d, n_span))

    def exists(dx, dy):
        ok = None
        for step, pos, size in ((dx, u, n_axial), (dy, t, n_span)):
            if step != 0:
                one = (pos + step >= 0) & (pos + step < size)
                ok = one if ok is None else ok & one
        return ok

    barrier = pltpu.get_barrier_semaphore()
    for dx, dy in DIRS:
        @pl.when(exists(dx, dy))
        def _(dx=dx, dy=dy):
            pl.semaphore_signal(barrier, inc=1, device_id=(u + dx, t + dy), device_id_type=MESH)
    for h in (0, 2, 3, 4, 5):
        pl.semaphore_signal(barrier, inc=1, device_id=sender(h), device_id_type=MESH)
    def span_of(pos, size):
        return 1 + (pos > 0).astype(jnp.int32) + (pos < size - 1).astype(jnp.int32)

    pl.semaphore_wait(barrier, span_of(u, n_axial) * span_of(t, n_span) + 4)

    def halo(k):
        dx, dy = DIRS[k]

        def xs(width):
            if dx == 1:
                return pl.ds(8 - width, width), pl.ds(4 - width, width)
            if dx == -1:
                return pl.ds(0, width), pl.ds(12, width)
            return pl.ds(0, 8), pl.ds(4, 8)

        ysrc, ydst = {1: (pl.ds(4, 4), pl.ds(12, 4)), -1: (pl.ds(0, 4), pl.ds(8, 4)), 0: (pl.ds(0, 8), pl.ds(0, 8))}[dy]
        sx, sxd = xs(4)
        rx, rxd = xs(3)
        target = (u + dx, t + dy)
        return (
            pltpu.make_async_remote_copy(
                stiff.at[sx, ysrc], s_ext.at[sxd, ydst], halo_send.at[k, 0], halo_recv.at[k, 0],
                device_id=target, device_id_type=MESH),
            pltpu.make_async_remote_copy(
                rhs.at[:, rx, ysrc], r_ext.at[:, rxd, ydst], halo_send.at[k, 1], halo_recv.at[k, 1],
                device_id=target, device_id_type=MESH),
        )

    for k, (dx, dy) in enumerate(DIRS):
        @pl.when(exists(dx, dy))
        def _(k=k):
            for copy in halo(k):
                copy.start()

    for load in loads[2:]:
        load.wait()
    cells = cell_v[...]
    slots = cells.shape[1]
    z_of = cells & 127
    row_of = lax.shift_right_logical(cells, 7)
    zhot[...] = jnp.where(
        lax.broadcasted_iota(jnp.int32, (128, slots), 0) == z_of, 1.0, 0.0
    ).astype(jnp.bfloat16)
    for e in range(8):
        r = (index_v[e] - (f - 1) * owned + 2 * NFFD) & (NFFD - 1)
        r = jnp.where(r >= NFFD // 2, r - NFFD // 2 + 3 * owned, r)
        hi = lax.shift_right_logical(r, owned.bit_length() - 1)
        low = r & (owned - 1)
        lohot[e] = jnp.where(
            lax.broadcasted_iota(jnp.int32, (lows, slots), 0) == low, 1.0, 0.0
        ).astype(jnp.bfloat16)
        mw[e] = jnp.where(
            lax.broadcasted_iota(jnp.int32, (8, slots), 0) == hi, weight_v[e], 0.0
        )
    loads[0].wait()
    loads[1].wait()

    for k, (dx, dy) in enumerate(DIRS):
        @pl.when(exists(-dx, -dy))
        def _(k=k):
            for copy in halo(k):
                copy.wait_recv()

    for c, n in chunks(0, 16):
        s = s_ext[c:c + n]
        sy = yshift(s, 1) + yshift(s, -1)
        sz = zshift(s, 1) + zshift(s, -1)
        syz = zshift(sy, 1) + zshift(sy, -1)
        p_ref[0, c:c + n] = 1.25 * s + 0.875 * (sy + sz) + 0.3125 * syz
        p_ref[1, c:c + n] = 1.25 * (sy + sz) + 0.875 * syz
    for c, n in chunks(1, 15):
        diag = p_ref[0, c - 1:c - 1 + n] + p_ref[0, c + 1:c + 1 + n] + p_ref[1, c:c + n]
        inv = jnp.where(s_ext[c:c + n] > 0, 1.0 / diag, 0.0)
        inv_ref[c:c + n] = inv
        q_ref[5, c:c + n] = diag
        for i in range(3):
            v_ref[i, c:c + n] = r_ext[i, c:c + n] * inv

    for sweep in range(SWEEPS):
        lo, hi = 2 + sweep, 14 - sweep
        for c, n in chunks(lo - 1, hi + 1):
            s = s_ext[c:c + n]
            ux, uy, uz = [s * v_ref[i, c:c + n] for i in range(3)]
            yp, ym = yshift(ux, 1), yshift(ux, -1)
            a = 2.0 * ux + (yp + ym)
            q_ref[1, c:c + n] = yp - ym
            p_ref[0, c:c + n] = 0.5 * a + 0.25 * (zshift(a, 1) + zshift(a, -1))
            q_ref[2, c:c + n] = zshift(ux, 1) - zshift(ux, -1)
            yp, ym = yshift(uy, 1), yshift(uy, -1)
            a = 2.0 * uy + (yp + ym)
            dy_uy = yp - ym
            p_ref[1, c:c + n] = 0.5 * a + 0.25 * (zshift(a, 1) + zshift(a, -1))
            q_ref[4, c:c + n] = zshift(dy_uy, 1) - zshift(dy_uy, -1)
            zp, zm = zshift(uz, 1), zshift(uz, -1)
            a = 2.0 * uz + (zp + zm)
            dz_uz = zp - zm
            p_ref[2, c:c + n] = 0.5 * a + 0.25 * (yshift(a, 1) + yshift(a, -1))
            q_ref[3, c:c + n] = yshift(dz_uz, 1) - yshift(dz_uz, -1)
            q_ref[0, c:c + n] = dy_uy + dz_uz
        for c, n in chunks(lo, hi):
            mid, up, down = slice(c, c + n), slice(c + 1, c + 1 + n), slice(c - 1, c - 1 + n)
            s = s_ext[mid]
            inv = inv_ref[mid]
            factor = q_ref[5, mid] + 2.0 * s
            cross = [
                q_ref[0, up] - q_ref[0, down],
                q_ref[1, up] - q_ref[1, down] + q_ref[3, mid],
                q_ref[2, up] - q_ref[2, down] + q_ref[4, mid],
            ]
            for i in range(3):
                v = v_ref[i, mid]
                smooth = p_ref[i, up] + p_ref[i, down] + 2.0 * p_ref[i, mid]
                av = factor * v - smooth - 0.25 * cross[i]
                new = v + (r_ext[i, mid] - av) * inv
                if sweep < SWEEPS - 1:
                    v_ref[i, mid] = new
                else:
                    own_v[i, c - 4:c - 4 + n] = new[:, 0:8]

    out = pltpu.make_async_copy(own_v, adj_out, local_sem.at[0])
    out.start()

    rows = own_v.shape[1] * own_v.shape[2]
    flat = own_v[...].reshape(3 * rows, 128)
    top = flat.astype(jnp.bfloat16)
    rest = (flat - top.astype(jnp.float32)).astype(jnp.bfloat16)
    at = jnp.dot(top, zhot[...], preferred_element_type=jnp.float32)
    at = at + jnp.dot(rest, zhot[...], preferred_element_type=jnp.float32)
    row_mask = lax.broadcasted_iota(jnp.int32, (rows, slots), 0) == row_of
    live_f = live_v[...].astype(jnp.float32)
    sens = []
    for i in range(3):
        picked = jnp.where(row_mask, at[i * rows:(i + 1) * rows], 0.0)
        adj_at = jnp.sum(picked, axis=0, keepdims=True)
        sens.append(live_f * (direct_v[i] - metric_v[i] * adj_at))
    total = jnp.zeros((48, lows), jnp.float32)
    for e in range(8):
        parts = jnp.concatenate([mw[e] * sens[i] for i in range(3)], axis=0)
        top = parts.astype(jnp.bfloat16).astype(jnp.float32)
        both = jnp.concatenate([top, parts - top], axis=0).astype(jnp.bfloat16)
        total = total + lax.dot_general(
            both, lohot[e], (((1,), (1,)), ((), ())), preferred_element_type=jnp.float32
        )
    total = total[0:24] + total[24:48]
    for h in range(6):
        for i in range(3):
            send_g[h, i:i + 1] = total[8 * i + h:8 * i + h + 1]

    sends = {
        h: pltpu.make_async_remote_copy(
            send_g.at[h], recv_g.at[h], g_send.at[h], g_recv.at[h],
            device_id=owner(h), device_id_type=MESH)
        for h in (0, 2, 3, 4, 5)
    }
    for copy in sends.values():
        copy.start()
    for k, (dx, dy) in enumerate(DIRS):
        @pl.when(exists(dx, dy))
        def _(k=k):
            for copy in halo(k):
                copy.wait_send()
    acc = send_g[1, 0:3]
    for h, copy in sends.items():
        copy.wait_recv()
        acc = acc + recv_g[h, 0:3]
    grad_v[...] = acc
    final = pltpu.make_async_copy(grad_v, grad_out, local_sem.at[1])
    final.start()
    for copy in sends.values():
        copy.wait_send()
    out.wait()
    final.wait()


def local(stiffness, adjoint_rhs, surf_cell, surf_live, ffd_index, ffd_weight, surf_direct, surf_metric):
    n_axial, n_span = lax.axis_size("axial"), lax.axis_size("span")
    owned = NFFD // (n_axial * n_span)
    lows = max(owned, 128)
    slots = surf_cell.shape[1]
    f32, i32 = jnp.float32, jnp.int32
    any_spec = pl.BlockSpec(memory_space=pl.ANY)
    dma = pltpu.SemaphoreType.DMA
    adjoint, grad = pl.pallas_call(
        functools.partial(kernel, n_axial, n_span),
        out_shape=(
            jax.ShapeDtypeStruct(adjoint_rhs.shape, f32),
            jax.ShapeDtypeStruct((3, lows), f32),
        ),
        in_specs=[any_spec] * 8,
        out_specs=(any_spec, any_spec),
        scratch_shapes=[
            pltpu.VMEM((16, 16, 128), f32),
            pltpu.VMEM((3, 16, 16, 128), f32),
            pltpu.VMEM((16, 16, 128), f32),
            pltpu.VMEM((3, 16, 16, 128), f32),
            pltpu.VMEM((3, 16, 16, 128), f32),
            pltpu.VMEM((6, 16, 16, 128), f32),
            pltpu.VMEM(adjoint_rhs.shape, f32),
            pltpu.VMEM(surf_cell.shape, i32),
            pltpu.VMEM(surf_live.shape, i32),
            pltpu.VMEM(ffd_index.shape, i32),
            pltpu.VMEM(ffd_weight.shape, f32),
            pltpu.VMEM(surf_direct.shape, f32),
            pltpu.VMEM(surf_metric.shape, f32),
            pltpu.VMEM((128, slots), jnp.bfloat16),
            pltpu.VMEM((8, lows, slots), jnp.bfloat16),
            pltpu.VMEM((8, 8, slots), f32),
            pltpu.VMEM((6, 8, lows), f32),
            pltpu.VMEM((6, 8, lows), f32),
            pltpu.VMEM((3, lows), f32),
            dma((8, 2)),
            dma((8, 2)),
            dma((6,)),
            dma((6,)),
            dma((8,)),
        ],
        compiler_params=pltpu.CompilerParams(collective_id=0, has_side_effects=True),
    )(stiffness, adjoint_rhs, surf_cell, surf_live, ffd_index, ffd_weight, surf_direct, surf_metric)
    return adjoint, grad[:, :owned].T


def solution(mesh):
    return jax.shard_map(
        local,
        mesh=mesh,
        in_specs=(
            P("axial", "span", None),
            P(None, "axial", "span", None),
            P("axial", "span"),
            P("axial", "span"),
            P(None, "axial", "span"),
            P(None, "axial", "span"),
            P(None, "axial", "span"),
            P(None, "axial", "span"),
        ),
        out_specs=(P(None, "axial", "span", None), P(("axial", "span"), None)),
        check_vma=False,
    )
```

```python
import functools

import jax
import jax.numpy as jnp
from jax import lax
from jax.experimental import pallas as pl
from jax.experimental.pallas import tpu as pltpu
from jax.sharding import PartitionSpec as P

SWEEPS = 3
NFFD = 4096
CHUNK = 2
MESH = pl.DeviceIdType.MESH
DIRS = [(dx, dy) for dx in (-1, 0, 1) for dy in (-1, 0, 1) if (dx, dy) != (0, 0)]


def yshift(a, step):
    return pltpu.roll(a, (-step) % 16, 1)


def zshift(a, step):
    return pltpu.roll(a, (-step) % 128, 2)


def chunks(lo, hi):
    return [(c, min(CHUNK, hi - c)) for c in range(lo, hi, CHUNK)]


def kernel(
    n_axial, n_span,
    stiff, rhs, cell, live, index, weight, direct, metric,
    adj_out, grad_out,
    s_ext, r_ext, inv_ref, v_ref, p_ref, q_ref,
    cell_v, live_v, index_v, weight_v, direct_v, metric_v,
    zhot, lohot, mw, send_g, recv_g,
    halo_send, halo_recv, g_send, g_recv, local_sem,
):
    u = lax.axis_index("axial")
    t = lax.axis_index("span")
    count = n_axial * n_span
    owned = NFFD // count
    f = u * n_span + t
    lows = lohot.shape[1]

    loads = [
        pltpu.make_async_copy(stiff, s_ext.at[pl.ds(4, 8), pl.ds(0, 8)], local_sem.at[0]),
        pltpu.make_async_copy(rhs, r_ext.at[:, pl.ds(4, 8), pl.ds(0, 8)], local_sem.at[1]),
        pltpu.make_async_copy(cell, cell_v, local_sem.at[2]),
        pltpu.make_async_copy(live, live_v, local_sem.at[3]),
        pltpu.make_async_copy(index, index_v, local_sem.at[4]),
        pltpu.make_async_copy(weight, weight_v, local_sem.at[5]),
        pltpu.make_async_copy(direct, direct_v, local_sem.at[6]),
        pltpu.make_async_copy(metric, metric_v, local_sem.at[7]),
    ]
    for load in loads[2:]:
        load.start()

    zero = jnp.zeros((8, 8, 128), jnp.float32)
    zero4 = jnp.zeros((4, 16, 128), jnp.float32)
    s_ext[0:4] = zero4
    s_ext[12:16] = zero4
    s_ext[4:12, 8:16] = zero
    for i in range(3):
        r_ext[i, 0:4] = zero4
        r_ext[i, 12:16] = zero4
        r_ext[i, 4:12, 8:16] = zero
    loads[0].start()
    loads[1].start()

    def owner(h):
        base = f + (count - 1) + h if h < 3 else f + (count - 1) + count // 2 + (h - 3)
        d = lax.rem(base, count)
        return (lax.div(d, n_span), lax.rem(d, n_span))

    def sender(h):
        base = f + count + 1 - h if h < 3 else f + count // 2 + count + 1 - (h - 3)
        d = lax.rem(base, count)
        return (lax.div(d, n_span), lax.rem(d, n_span))

    def exists(dx, dy):
        ok = None
        for step, pos, size in ((dx, u, n_axial), (dy, t, n_span)):
            if step != 0:
                one = (pos + step >= 0) & (pos + step < size)
                ok = one if ok is None else ok & one
        return ok

    barrier = pltpu.get_barrier_semaphore()
    for dx, dy in DIRS:
        @pl.when(exists(dx, dy))
        def _(dx=dx, dy=dy):
            pl.semaphore_signal(barrier, inc=1, device_id=(u + dx, t + dy), device_id_type=MESH)
    for h in (0, 2, 3, 4, 5):
        pl.semaphore_signal(barrier, inc=1, device_id=sender(h), device_id_type=MESH)
    def span_of(pos, size):
        return 1 + (pos > 0).astype(jnp.int32) + (pos < size - 1).astype(jnp.int32)

    loads[0].wait()
    loads[1].wait()
    pl.semaphore_wait(barrier, span_of(u, n_axial) * span_of(t, n_span) + 4)

    def halo(k):
        dx, dy = DIRS[k]

        def xs(width):
            if dx == 1:
                return pl.ds(12 - width, width), pl.ds(4 - width, width)
            if dx == -1:
                return pl.ds(4, width), pl.ds(12, width)
            return pl.ds(4, 8), pl.ds(4, 8)

        ysrc, ydst = {1: (pl.ds(4, 4), pl.ds(12, 4)), -1: (pl.ds(0, 4), pl.ds(8, 4)), 0: (pl.ds(0, 8), pl.ds(0, 8))}[dy]
        sx, sxd = xs(4)
        rx, rxd = xs(3)
        target = (u + dx, t + dy)
        return (
            pltpu.make_async_remote_copy(
                s_ext.at[sx, ysrc], s_ext.at[sxd, ydst], halo_send.at[k, 0], halo_recv.at[k, 0],
                device_id=target, device_id_type=MESH),
            pltpu.make_async_remote_copy(
                r_ext.at[:, rx, ysrc], r_ext.at[:, rxd, ydst], halo_send.at[k, 1], halo_recv.at[k, 1],
                device_id=target, device_id_type=MESH),
        )

    for k, (dx, dy) in enumerate(DIRS):
        @pl.when(exists(dx, dy))
        def _(k=k):
            for copy in halo(k):
                copy.start()

    for load in loads[2:]:
        load.wait()
    cells = cell_v[...]
    slots = cells.shape[1]
    z_of = cells & 127
    row_of = lax.shift_right_logical(cells, 7)
    zhot[...] = jnp.where(
        lax.broadcasted_iota(jnp.int32, (128, slots), 0) == z_of, 1.0, 0.0
    ).astype(jnp.bfloat16)
    for e in range(8):
        r = (index_v[e] - (f - 1) * owned + 2 * NFFD) & (NFFD - 1)
        r = jnp.where(r >= NFFD // 2, r - NFFD // 2 + 3 * owned, r)
        hi = lax.shift_right_logical(r, owned.bit_length() - 1)
        low = r & (owned - 1)
        lohot[e] = jnp.where(
            lax.broadcasted_iota(jnp.int32, (lows, slots), 0) == low, 1.0, 0.0
        ).astype(jnp.bfloat16)
        mw[e] = jnp.where(
            lax.broadcasted_iota(jnp.int32, (8, slots), 0) == hi, weight_v[e], 0.0
        )

    for k, (dx, dy) in enumerate(DIRS):
        @pl.when(exists(-dx, -dy))
        def _(k=k):
            for copy in halo(k):
                copy.wait_recv()

    for c, n in chunks(0, 16):
        s = s_ext[c:c + n]
        sy = yshift(s, 1) + yshift(s, -1)
        sz = zshift(s, 1) + zshift(s, -1)
        syz = zshift(sy, 1) + zshift(sy, -1)
        p_ref[0, c:c + n] = 1.25 * s + 0.875 * (sy + sz) + 0.3125 * syz
        p_ref[1, c:c + n] = 1.25 * (sy + sz) + 0.875 * syz
    for c, n in chunks(1, 15):
        diag = p_ref[0, c - 1:c - 1 + n] + p_ref[0, c + 1:c + 1 + n] + p_ref[1, c:c + n]
        inv = jnp.where(s_ext[c:c + n] > 0, 1.0 / diag, 0.0)
        inv_ref[c:c + n] = inv
        q_ref[5, c:c + n] = diag
        for i in range(3):
            v_ref[i, c:c + n] = r_ext[i, c:c + n] * inv

    for sweep in range(SWEEPS):
        lo, hi = 2 + sweep, 14 - sweep
        for c, n in chunks(lo - 1, hi + 1):
            s = s_ext[c:c + n]
            ux, uy, uz = [s * v_ref[i, c:c + n] for i in range(3)]
            yp, ym = yshift(ux, 1), yshift(ux, -1)
            a = 2.0 * ux + (yp + ym)
            q_ref[1, c:c + n] = yp - ym
            p_ref[0, c:c + n] = 0.5 * a + 0.25 * (zshift(a, 1) + zshift(a, -1))
            q_ref[2, c:c + n] = zshift(ux, 1) - zshift(ux, -1)
            yp, ym = yshift(uy, 1), yshift(uy, -1)
            a = 2.0 * uy + (yp + ym)
            dy_uy = yp - ym
            p_ref[1, c:c + n] = 0.5 * a + 0.25 * (zshift(a, 1) + zshift(a, -1))
            q_ref[4, c:c + n] = zshift(dy_uy, 1) - zshift(dy_uy, -1)
            zp, zm = zshift(uz, 1), zshift(uz, -1)
            a = 2.0 * uz + (zp + zm)
            dz_uz = zp - zm
            p_ref[2, c:c + n] = 0.5 * a + 0.25 * (yshift(a, 1) + yshift(a, -1))
            q_ref[3, c:c + n] = yshift(dz_uz, 1) - yshift(dz_uz, -1)
            q_ref[0, c:c + n] = dy_uy + dz_uz
        for c, n in chunks(lo, hi):
            mid, up, down = slice(c, c + n), slice(c + 1, c + 1 + n), slice(c - 1, c - 1 + n)
            s = s_ext[mid]
            inv = inv_ref[mid]
            factor = q_ref[5, mid] + 2.0 * s
            cross = [
                q_ref[0, up] - q_ref[0, down],
                q_ref[1, up] - q_ref[1, down] + q_ref[3, mid],
                q_ref[2, up] - q_ref[2, down] + q_ref[4, mid],
            ]
            for i in range(3):
                v = v_ref[i, mid]
                smooth = p_ref[i, up] + p_ref[i, down] + 2.0 * p_ref[i, mid]
                av = factor * v - smooth - 0.25 * cross[i]
                new = v + (r_ext[i, mid] - av) * inv
                if sweep < SWEEPS - 1:
                    v_ref[i, mid] = new
                else:
                    adj_out[i, c - 4:c - 4 + n] = new[:, 0:8]

    rows = adj_out.shape[1] * adj_out.shape[2]
    flat = adj_out[...].reshape(3 * rows, 128)
    top = flat.astype(jnp.bfloat16)
    rest = (flat - top.astype(jnp.float32)).astype(jnp.bfloat16)
    at = jnp.dot(top, zhot[...], preferred_element_type=jnp.float32)
    at = at + jnp.dot(rest, zhot[...], preferred_element_type=jnp.float32)
    row_mask = lax.broadcasted_iota(jnp.int32, (rows, slots), 0) == row_of
    live_f = live_v[...].astype(jnp.float32)
    sens = []
    for i in range(3):
        picked = jnp.where(row_mask, at[i * rows:(i + 1) * rows], 0.0)
        adj_at = jnp.sum(picked, axis=0, keepdims=True)
        sens.append(live_f * (direct_v[i] - metric_v[i] * adj_at))
    total = jnp.zeros((48, lows), jnp.float32)
    for e in range(8):
        parts = jnp.concatenate([mw[e] * sens[i] for i in range(3)], axis=0)
        top = parts.astype(jnp.bfloat16).astype(jnp.float32)
        both = jnp.concatenate([top, parts - top], axis=0).astype(jnp.bfloat16)
        total = total + lax.dot_general(
            both, lohot[e], (((1,), (1,)), ((), ())), preferred_element_type=jnp.float32
        )
    total = total[0:24] + total[24:48]
    for h in range(6):
        for i in range(3):
            send_g[h, i:i + 1] = total[8 * i + h:8 * i + h + 1]

    sends = {
        h: pltpu.make_async_remote_copy(
            send_g.at[h], recv_g.at[h], g_send.at[h], g_recv.at[h],
            device_id=owner(h), device_id_type=MESH)
        for h in (0, 2, 3, 4, 5)
    }
    for copy in sends.values():
        copy.start()
    for k, (dx, dy) in enumerate(DIRS):
        @pl.when(exists(dx, dy))
        def _(k=k):
            for copy in halo(k):
                copy.wait_send()
    acc = send_g[1, 0:3]
    for h, copy in sends.items():
        copy.wait_recv()
        acc = acc + recv_g[h, 0:3]
    grad_out[...] = acc
    for copy in sends.values():
        copy.wait_send()


def write(adj, grad, adj_hbm, grad_hbm, sem):
    copies = [
        pltpu.make_async_copy(adj, adj_hbm, sem.at[0]),
        pltpu.make_async_copy(grad, grad_hbm, sem.at[1]),
    ]
    for copy in copies:
        copy.start()
    for copy in copies:
        copy.wait()


def local(stiffness, adjoint_rhs, surf_cell, surf_live, ffd_index, ffd_weight, surf_direct, surf_metric):
    n_axial, n_span = lax.axis_size("axial"), lax.axis_size("span")
    owned = NFFD // (n_axial * n_span)
    lows = max(owned, 128)
    slots = surf_cell.shape[1]
    f32, i32 = jnp.float32, jnp.int32
    any_spec = pl.BlockSpec(memory_space=pl.ANY)
    dma = pltpu.SemaphoreType.DMA
    adjoint, grad = pl.pallas_call(
        functools.partial(kernel, n_axial, n_span),
        out_shape=(
            pltpu.VMEM(adjoint_rhs.shape, f32),
            pltpu.VMEM((3, lows), f32),
        ),
        in_specs=[any_spec] * 8,
        out_specs=(pl.BlockSpec(memory_space=pltpu.VMEM),) * 2,
        scratch_shapes=[
            pltpu.VMEM((16, 16, 128), f32),
            pltpu.VMEM((3, 16, 16, 128), f32),
            pltpu.VMEM((16, 16, 128), f32),
            pltpu.VMEM((3, 16, 16, 128), f32),
            pltpu.VMEM((3, 16, 16, 128), f32),
            pltpu.VMEM((6, 16, 16, 128), f32),
            pltpu.VMEM(surf_cell.shape, i32),
            pltpu.VMEM(surf_live.shape, i32),
            pltpu.VMEM(ffd_index.shape, i32),
            pltpu.VMEM(ffd_weight.shape, f32),
            pltpu.VMEM(surf_direct.shape, f32),
            pltpu.VMEM(surf_metric.shape, f32),
            pltpu.VMEM((128, slots), jnp.bfloat16),
            pltpu.VMEM((8, lows, slots), jnp.bfloat16),
            pltpu.VMEM((8, 8, slots), f32),
            pltpu.VMEM((6, 8, lows), f32),
            pltpu.VMEM((6, 8, lows), f32),
            dma((8, 2)),
            dma((8, 2)),
            dma((6,)),
            dma((6,)),
            dma((8,)),
        ],
        compiler_params=pltpu.CompilerParams(collective_id=0, has_side_effects=True),
    )(stiffness, adjoint_rhs, surf_cell, surf_live, ffd_index, ffd_weight, surf_direct, surf_metric)
    vmem_spec = pl.BlockSpec(memory_space=pltpu.VMEM)
    adjoint, grad = pl.pallas_call(
        write,
        out_shape=(
            jax.ShapeDtypeStruct(adjoint_rhs.shape, f32),
            jax.ShapeDtypeStruct((3, lows), f32),
        ),
        in_specs=[vmem_spec] * 2,
        out_specs=(any_spec, any_spec),
        scratch_shapes=[dma((2,))],
    )(*(pltpu.with_memory_space_constraint(a, pltpu.VMEM) for a in (adjoint, grad)))
    return adjoint, grad[:, :owned].T


def solution(mesh):
    return jax.shard_map(
        local,
        mesh=mesh,
        in_specs=(
            P("axial", "span", None),
            P(None, "axial", "span", None),
            P("axial", "span"),
            P("axial", "span"),
            P(None, "axial", "span"),
            P(None, "axial", "span"),
            P(None, "axial", "span"),
            P(None, "axial", "span"),
        ),
        out_specs=(P(None, "axial", "span", None), P(("axial", "span"), None)),
        check_vma=False,
    )
```

```python
import functools

import jax
import jax.numpy as jnp
from jax import lax
from jax.experimental import pallas as pl
from jax.experimental.pallas import tpu as pltpu
from jax.sharding import PartitionSpec as P

SWEEPS = 3
NFFD = 4096
CHUNK = 2
MESH = pl.DeviceIdType.MESH
DIRS = [(0, 1), (0, -1), (1, 1), (1, -1), (-1, 1), (-1, -1), (1, 0), (-1, 0)]


def yshift(a, step):
    return pltpu.roll(a, (-step) % 16, 1)


def zshift(a, step):
    return pltpu.roll(a, (-step) % 128, 2)


def chunks(lo, hi):
    return [(c, min(CHUNK, hi - c)) for c in range(lo, hi, CHUNK)]


def kernel(
    n_axial, n_span,
    stiff, rhs, cell, live, index, weight, direct, metric,
    adj_out, grad_out,
    s_ext, r_ext, inv_ref, v_ref, p_ref, q_ref,
    cell_v, live_v, index_v, weight_v, direct_v, metric_v,
    zhot, lohot, mw, send_g, recv_g,
    halo_send, halo_recv, g_send, g_recv, local_sem,
):
    u = lax.axis_index("axial")
    t = lax.axis_index("span")
    count = n_axial * n_span
    owned = NFFD // count
    f = u * n_span + t
    lows = lohot.shape[1]

    loads = [
        pltpu.make_async_copy(stiff, s_ext.at[pl.ds(4, 8), pl.ds(0, 8)], local_sem.at[0]),
        pltpu.make_async_copy(rhs, r_ext.at[:, pl.ds(4, 8), pl.ds(0, 8)], local_sem.at[1]),
        pltpu.make_async_copy(cell, cell_v, local_sem.at[2]),
        pltpu.make_async_copy(live, live_v, local_sem.at[3]),
        pltpu.make_async_copy(index, index_v, local_sem.at[4]),
        pltpu.make_async_copy(weight, weight_v, local_sem.at[5]),
        pltpu.make_async_copy(direct, direct_v, local_sem.at[6]),
        pltpu.make_async_copy(metric, metric_v, local_sem.at[7]),
    ]
    for load in loads:
        load.start()

    def owner(h):
        base = f + (count - 1) + h if h < 3 else f + (count - 1) + count // 2 + (h - 3)
        d = lax.rem(base, count)
        return (lax.div(d, n_span), lax.rem(d, n_span))

    def sender(h):
        base = f + count + 1 - h if h < 3 else f + count // 2 + count + 1 - (h - 3)
        d = lax.rem(base, count)
        return (lax.div(d, n_span), lax.rem(d, n_span))

    def exists(dx, dy):
        ok = None
        for step, pos, size in ((dx, u, n_axial), (dy, t, n_span)):
            if step != 0:
                one = (pos + step >= 0) & (pos + step < size)
                ok = one if ok is None else ok & one
        return ok

    barrier = pltpu.get_barrier_semaphore()
    for h in (0, 2, 3, 4, 5):
        pl.semaphore_signal(barrier, inc=1, device_id=sender(h), device_id_type=MESH)
    for dx, dy in DIRS:
        @pl.when(exists(dx, dy))
        def _(dx=dx, dy=dy):
            pl.semaphore_signal(barrier, inc=1, device_id=(u + dx, t + dy), device_id_type=MESH)
    def region(dx, dy):
        xs = {0: slice(4, 12), 1: slice(12, 16), -1: slice(0, 4)}[dx]
        ys = {0: slice(0, 8), 1: slice(8, 12), -1: slice(12, 16)}[dy]
        return xs, ys

    for dx, dy in DIRS:
        @pl.when(jnp.logical_not(exists(dx, dy)))
        def _(dx=dx, dy=dy):
            xs, ys = region(dx, dy)
            zero = jnp.zeros((xs.stop - xs.start, ys.stop - ys.start, 128), jnp.float32)
            s_ext[xs, ys] = zero
            for i in range(3):
                r_ext[i, xs, ys] = zero

    def span_of(pos, size):
        return 1 + (pos > 0).astype(jnp.int32) + (pos < size - 1).astype(jnp.int32)

    loads[0].wait()
    loads[1].wait()
    pl.semaphore_wait(barrier, span_of(u, n_axial) * span_of(t, n_span) + 4)

    def halo(k):
        dx, dy = DIRS[k]

        def xs(width):
            if dx == 1:
                return pl.ds(12 - width, width), pl.ds(4 - width, width)
            if dx == -1:
                return pl.ds(4, width), pl.ds(12, width)
            return pl.ds(4, 8), pl.ds(4, 8)

        def ys(width):
            if dy == 1:
                return pl.ds(8 - width, width), pl.ds(16 - width, width)
            if dy == -1:
                return pl.ds(0, width), pl.ds(8, width)
            return pl.ds(0, 8), pl.ds(0, 8)

        sx, sxd = xs(4)
        rx, rxd = xs(3)
        sy, syd = ys(4)
        ry, ryd = ys(3)
        target = (u + dx, t + dy)
        return (
            pltpu.make_async_remote_copy(
                s_ext.at[sx, sy], s_ext.at[sxd, syd], halo_send.at[k, 0], halo_recv.at[k, 0],
                device_id=target, device_id_type=MESH),
            pltpu.make_async_remote_copy(
                r_ext.at[:, rx, ry], r_ext.at[:, rxd, ryd], halo_send.at[k, 1], halo_recv.at[k, 1],
                device_id=target, device_id_type=MESH),
        )

    for k, (dx, dy) in enumerate(DIRS):
        @pl.when(exists(dx, dy))
        def _(k=k):
            for copy in halo(k):
                copy.start()

    for load in loads[2:]:
        load.wait()
    cells = cell_v[...]
    slots = cells.shape[1]
    z_of = cells & 127
    row_of = lax.shift_right_logical(cells, 7)
    zhot[...] = jnp.where(
        lax.broadcasted_iota(jnp.int32, (128, slots), 0) == z_of, 1.0, 0.0
    ).astype(jnp.bfloat16)
    for e in range(8):
        r = (index_v[e] - (f - 1) * owned + 2 * NFFD) & (NFFD - 1)
        r = jnp.where(r >= NFFD // 2, r - NFFD // 2 + 3 * owned, r)
        hi = lax.shift_right_logical(r, owned.bit_length() - 1)
        low = r & (owned - 1)
        lohot[e] = jnp.where(
            lax.broadcasted_iota(jnp.int32, (lows, slots), 0) == low, 1.0, 0.0
        ).astype(jnp.bfloat16)
        mw[e] = jnp.where(
            lax.broadcasted_iota(jnp.int32, (8, slots), 0) == hi, weight_v[e], 0.0
        )

    for k, (dx, dy) in enumerate(DIRS):
        @pl.when(exists(-dx, -dy))
        def _(k=k):
            for copy in halo(k):
                copy.wait_recv()

    for c, n in chunks(0, 16):
        s = s_ext[c:c + n]
        sy = yshift(s, 1) + yshift(s, -1)
        sz = zshift(s, 1) + zshift(s, -1)
        syz = zshift(sy, 1) + zshift(sy, -1)
        p_ref[0, c:c + n] = 1.25 * s + 0.875 * (sy + sz) + 0.3125 * syz
        p_ref[1, c:c + n] = 1.25 * (sy + sz) + 0.875 * syz
    for c, n in chunks(1, 15):
        diag = p_ref[0, c - 1:c - 1 + n] + p_ref[0, c + 1:c + 1 + n] + p_ref[1, c:c + n]
        inv = jnp.where(s_ext[c:c + n] > 0, 1.0 / diag, 0.0)
        inv_ref[c:c + n] = inv
        q_ref[5, c:c + n] = diag
        for i in range(3):
            v_ref[i, c:c + n] = r_ext[i, c:c + n] * inv

    for sweep in range(SWEEPS):
        lo, hi = 2 + sweep, 14 - sweep
        for c, n in chunks(lo - 1, hi + 1):
            s = s_ext[c:c + n]
            ux, uy, uz = [s * v_ref[i, c:c + n] for i in range(3)]
            yp, ym = yshift(ux, 1), yshift(ux, -1)
            a = 2.0 * ux + (yp + ym)
            q_ref[1, c:c + n] = yp - ym
            p_ref[0, c:c + n] = 0.5 * a + 0.25 * (zshift(a, 1) + zshift(a, -1))
            q_ref[2, c:c + n] = zshift(ux, 1) - zshift(ux, -1)
            yp, ym = yshift(uy, 1), yshift(uy, -1)
            a = 2.0 * uy + (yp + ym)
            dy_uy = yp - ym
            p_ref[1, c:c + n] = 0.5 * a + 0.25 * (zshift(a, 1) + zshift(a, -1))
            q_ref[4, c:c + n] = zshift(dy_uy, 1) - zshift(dy_uy, -1)
            zp, zm = zshift(uz, 1), zshift(uz, -1)
            a = 2.0 * uz + (zp + zm)
            dz_uz = zp - zm
            p_ref[2, c:c + n] = 0.5 * a + 0.25 * (yshift(a, 1) + yshift(a, -1))
            q_ref[3, c:c + n] = yshift(dz_uz, 1) - yshift(dz_uz, -1)
            q_ref[0, c:c + n] = dy_uy + dz_uz
        for c, n in chunks(lo, hi):
            mid, up, down = slice(c, c + n), slice(c + 1, c + 1 + n), slice(c - 1, c - 1 + n)
            s = s_ext[mid]
            inv = inv_ref[mid]
            factor = q_ref[5, mid] + 2.0 * s
            cross = [
                q_ref[0, up] - q_ref[0, down],
                q_ref[1, up] - q_ref[1, down] + q_ref[3, mid],
                q_ref[2, up] - q_ref[2, down] + q_ref[4, mid],
            ]
            for i in range(3):
                v = v_ref[i, mid]
                smooth = p_ref[i, up] + p_ref[i, down] + 2.0 * p_ref[i, mid]
                av = factor * v - smooth - 0.25 * cross[i]
                new = v + (r_ext[i, mid] - av) * inv
                if sweep < SWEEPS - 1:
                    v_ref[i, mid] = new
                else:
                    adj_out[i, c - 4:c - 4 + n] = new[:, 0:8]

    rows = adj_out.shape[1] * adj_out.shape[2]
    flat = adj_out[...].reshape(3 * rows, 128)
    top = flat.astype(jnp.bfloat16)
    rest = (flat - top.astype(jnp.float32)).astype(jnp.bfloat16)
    at = jnp.dot(top, zhot[...], preferred_element_type=jnp.float32)
    at = at + jnp.dot(rest, zhot[...], preferred_element_type=jnp.float32)
    row_mask = lax.broadcasted_iota(jnp.int32, (rows, slots), 0) == row_of
    live_f = live_v[...].astype(jnp.float32)
    sens = []
    for i in range(3):
        picked = jnp.where(row_mask, at[i * rows:(i + 1) * rows], 0.0)
        adj_at = jnp.sum(picked, axis=0, keepdims=True)
        sens.append(live_f * (direct_v[i] - metric_v[i] * adj_at))
    total = jnp.zeros((48, lows), jnp.float32)
    for e in range(8):
        parts = jnp.concatenate([mw[e] * sens[i] for i in range(3)], axis=0)
        top = parts.astype(jnp.bfloat16).astype(jnp.float32)
        both = jnp.concatenate([top, parts - top], axis=0).astype(jnp.bfloat16)
        total = total + lax.dot_general(
            both, lohot[e], (((1,), (1,)), ((), ())), preferred_element_type=jnp.float32
        )
    total = total[0:24] + total[24:48]
    for h in range(6):
        for i in range(3):
            send_g[h, i:i + 1] = total[8 * i + h:8 * i + h + 1]

    sends = {
        h: pltpu.make_async_remote_copy(
            send_g.at[h], recv_g.at[h], g_send.at[h], g_recv.at[h],
            device_id=owner(h), device_id_type=MESH)
        for h in (0, 2, 3, 4, 5)
    }
    for copy in sends.values():
        copy.start()
    for k, (dx, dy) in enumerate(DIRS):
        @pl.when(exists(dx, dy))
        def _(k=k):
            for copy in halo(k):
                copy.wait_send()
    acc = send_g[1, 0:3]
    for h, copy in sends.items():
        copy.wait_recv()
        acc = acc + recv_g[h, 0:3]
    grad_out[...] = acc
    for copy in sends.values():
        copy.wait_send()


def write(adj, grad, adj_hbm, grad_hbm, sem):
    copies = [
        pltpu.make_async_copy(adj, adj_hbm, sem.at[0]),
        pltpu.make_async_copy(grad, grad_hbm, sem.at[1]),
    ]
    for copy in copies:
        copy.start()
    for copy in copies:
        copy.wait()


def local(stiffness, adjoint_rhs, surf_cell, surf_live, ffd_index, ffd_weight, surf_direct, surf_metric):
    n_axial, n_span = lax.axis_size("axial"), lax.axis_size("span")
    owned = NFFD // (n_axial * n_span)
    lows = max(owned, 128)
    slots = surf_cell.shape[1]
    f32, i32 = jnp.float32, jnp.int32
    any_spec = pl.BlockSpec(memory_space=pl.ANY)
    dma = pltpu.SemaphoreType.DMA
    adjoint, grad = pl.pallas_call(
        functools.partial(kernel, n_axial, n_span),
        out_shape=(
            pltpu.VMEM(adjoint_rhs.shape, f32),
            pltpu.VMEM((3, lows), f32),
        ),
        in_specs=[any_spec] * 8,
        out_specs=(pl.BlockSpec(memory_space=pltpu.VMEM),) * 2,
        scratch_shapes=[
            pltpu.VMEM((16, 16, 128), f32),
            pltpu.VMEM((3, 16, 16, 128), f32),
            pltpu.VMEM((16, 16, 128), f32),
            pltpu.VMEM((3, 16, 16, 128), f32),
            pltpu.VMEM((3, 16, 16, 128), f32),
            pltpu.VMEM((6, 16, 16, 128), f32),
            pltpu.VMEM(surf_cell.shape, i32),
            pltpu.VMEM(surf_live.shape, i32),
            pltpu.VMEM(ffd_index.shape, i32),
            pltpu.VMEM(ffd_weight.shape, f32),
            pltpu.VMEM(surf_direct.shape, f32),
            pltpu.VMEM(surf_metric.shape, f32),
            pltpu.VMEM((128, slots), jnp.bfloat16),
            pltpu.VMEM((8, lows, slots), jnp.bfloat16),
            pltpu.VMEM((8, 8, slots), f32),
            pltpu.VMEM((6, 8, lows), f32),
            pltpu.VMEM((6, 8, lows), f32),
            dma((8, 2)),
            dma((8, 2)),
            dma((6,)),
            dma((6,)),
            dma((8,)),
        ],
        compiler_params=pltpu.CompilerParams(collective_id=0, has_side_effects=True),
    )(stiffness, adjoint_rhs, surf_cell, surf_live, ffd_index, ffd_weight, surf_direct, surf_metric)
    vmem_spec = pl.BlockSpec(memory_space=pltpu.VMEM)
    adjoint, grad = pl.pallas_call(
        write,
        out_shape=(
            jax.ShapeDtypeStruct(adjoint_rhs.shape, f32),
            jax.ShapeDtypeStruct((3, lows), f32),
        ),
        in_specs=[vmem_spec] * 2,
        out_specs=(any_spec, any_spec),
        scratch_shapes=[dma((2,))],
    )(*(pltpu.with_memory_space_constraint(a, pltpu.VMEM) for a in (adjoint, grad)))
    return adjoint, grad[:, :owned].T


def solution(mesh):
    return jax.shard_map(
        local,
        mesh=mesh,
        in_specs=(
            P("axial", "span", None),
            P(None, "axial", "span", None),
            P("axial", "span"),
            P("axial", "span"),
            P(None, "axial", "span"),
            P(None, "axial", "span"),
            P(None, "axial", "span"),
            P(None, "axial", "span"),
        ),
        out_specs=(P(None, "axial", "span", None), P(("axial", "span"), None)),
        check_vma=False,
    )
```

```python
import functools

import jax
import jax.numpy as jnp
from jax import lax
from jax.experimental import pallas as pl
from jax.experimental.pallas import tpu as pltpu
from jax.sharding import PartitionSpec as P

SWEEPS = 3
NFFD = 4096
CHUNK = 2
MESH = pl.DeviceIdType.MESH
DIRS = [(0, 1), (0, -1), (1, 1), (1, -1), (-1, 1), (-1, -1), (1, 0), (-1, 0)]


def yshift(a, step):
    return pltpu.roll(a, (-step) % 16, 1)


def zshift(a, step):
    return pltpu.roll(a, (-step) % 128, 2)


def chunks(lo, hi):
    return [(c, min(CHUNK, hi - c)) for c in range(lo, hi, CHUNK)]


def kernel(
    n_axial, n_span,
    stiff, rhs, cell, live, index, weight, direct, metric,
    adj_out, grad_out,
    s_ext, r_ext, inv_ref, v_ref, p_ref, q_ref,
    cell_v, live_v, index_v, weight_v, direct_v, metric_v,
    zhot, lohot, mw, send_g, recv_g,
    halo_send, halo_recv, g_send, g_recv, local_sem,
):
    u = lax.axis_index("axial")
    t = lax.axis_index("span")
    count = n_axial * n_span
    owned = NFFD // count
    f = u * n_span + t
    lows = lohot.shape[1]

    loads = [
        pltpu.make_async_copy(stiff, s_ext.at[pl.ds(4, 8), pl.ds(0, 8)], local_sem.at[0]),
        pltpu.make_async_copy(rhs, r_ext.at[:, pl.ds(4, 8), pl.ds(0, 8)], local_sem.at[1]),
        pltpu.make_async_copy(cell, cell_v, local_sem.at[2]),
        pltpu.make_async_copy(live, live_v, local_sem.at[3]),
        pltpu.make_async_copy(index, index_v, local_sem.at[4]),
        pltpu.make_async_copy(weight, weight_v, local_sem.at[5]),
        pltpu.make_async_copy(direct, direct_v, local_sem.at[6]),
        pltpu.make_async_copy(metric, metric_v, local_sem.at[7]),
    ]
    for load in loads:
        load.start()

    def owner(h):
        base = f + (count - 1) + h if h < 3 else f + (count - 1) + count // 2 + (h - 3)
        d = lax.rem(base, count)
        return (lax.div(d, n_span), lax.rem(d, n_span))

    def sender(h):
        base = f + count + 1 - h if h < 3 else f + count // 2 + count + 1 - (h - 3)
        d = lax.rem(base, count)
        return (lax.div(d, n_span), lax.rem(d, n_span))

    def exists(dx, dy):
        ok = None
        for step, pos, size in ((dx, u, n_axial), (dy, t, n_span)):
            if step != 0:
                one = (pos + step >= 0) & (pos + step < size)
                ok = one if ok is None else ok & one
        return ok

    barrier = pltpu.get_barrier_semaphore()
    for h in (0, 2, 3, 4, 5):
        pl.semaphore_signal(barrier, inc=1, device_id=sender(h), device_id_type=MESH)
    for dx, dy in DIRS:
        @pl.when(exists(dx, dy))
        def _(dx=dx, dy=dy):
            pl.semaphore_signal(barrier, inc=1, device_id=(u + dx, t + dy), device_id_type=MESH)
    def region(dx, dy):
        xs = {0: slice(4, 12), 1: slice(12, 16), -1: slice(0, 4)}[dx]
        ys = {0: slice(0, 8), 1: slice(8, 12), -1: slice(12, 16)}[dy]
        return xs, ys

    for dx, dy in DIRS:
        @pl.when(jnp.logical_not(exists(dx, dy)))
        def _(dx=dx, dy=dy):
            xs, ys = region(dx, dy)
            zero = jnp.zeros((xs.stop - xs.start, ys.stop - ys.start, 128), jnp.float32)
            s_ext[xs, ys] = zero
            for i in range(3):
                r_ext[i, xs, ys] = zero

    def span_of(pos, size):
        return 1 + (pos > 0).astype(jnp.int32) + (pos < size - 1).astype(jnp.int32)

    loads[0].wait()
    loads[1].wait()
    pl.semaphore_wait(barrier, span_of(u, n_axial) * span_of(t, n_span) + 4)

    def halo(k):
        dx, dy = DIRS[k]

        def xs(width):
            if dx == 1:
                return pl.ds(12 - width, width), pl.ds(4 - width, width)
            if dx == -1:
                return pl.ds(4, width), pl.ds(12, width)
            return pl.ds(4, 8), pl.ds(4, 8)

        def ys(width):
            if dy == 1:
                return pl.ds(8 - width, width), pl.ds(16 - width, width)
            if dy == -1:
                return pl.ds(0, width), pl.ds(8, width)
            return pl.ds(0, 8), pl.ds(0, 8)

        sx, sxd = xs(4)
        rx, rxd = xs(3)
        sy, syd = ys(4)
        ry, ryd = ys(3)
        target = (u + dx, t + dy)
        return (
            pltpu.make_async_remote_copy(
                s_ext.at[sx, sy], s_ext.at[sxd, syd], halo_send.at[k, 0], halo_recv.at[k, 0],
                device_id=target, device_id_type=MESH),
            pltpu.make_async_remote_copy(
                r_ext.at[:, rx, ry], r_ext.at[:, rxd, ryd], halo_send.at[k, 1], halo_recv.at[k, 1],
                device_id=target, device_id_type=MESH),
        )

    for piece in range(2):
        for k, (dx, dy) in enumerate(DIRS):
            @pl.when(exists(dx, dy))
            def _(k=k, piece=piece):
                halo(k)[piece].start()

    for load in loads[2:]:
        load.wait()
    cells = cell_v[...]
    slots = cells.shape[1]
    z_of = cells & 127
    row_of = lax.shift_right_logical(cells, 7)
    zhot[...] = jnp.where(
        lax.broadcasted_iota(jnp.int32, (128, slots), 0) == z_of, 1.0, 0.0
    ).astype(jnp.bfloat16)
    for e in range(8):
        r = (index_v[e] - (f - 1) * owned + 2 * NFFD) & (NFFD - 1)
        r = jnp.where(r >= NFFD // 2, r - NFFD // 2 + 3 * owned, r)
        hi = lax.shift_right_logical(r, owned.bit_length() - 1)
        low = r & (owned - 1)
        lohot[e] = jnp.where(
            lax.broadcasted_iota(jnp.int32, (lows, slots), 0) == low, 1.0, 0.0
        ).astype(jnp.bfloat16)
        mw[e] = jnp.where(
            lax.broadcasted_iota(jnp.int32, (8, slots), 0) == hi, weight_v[e], 0.0
        )

    def arrived(piece):
        for k, (dx, dy) in enumerate(DIRS):
            @pl.when(exists(-dx, -dy))
            def _(k=k):
                halo(k)[piece].wait_recv()

    arrived(0)

    for c, n in chunks(0, 16):
        s = s_ext[c:c + n]
        sy = yshift(s, 1) + yshift(s, -1)
        sz = zshift(s, 1) + zshift(s, -1)
        syz = zshift(sy, 1) + zshift(sy, -1)
        p_ref[0, c:c + n] = 1.25 * s + 0.875 * (sy + sz) + 0.3125 * syz
        p_ref[1, c:c + n] = 1.25 * (sy + sz) + 0.875 * syz
    for c, n in chunks(1, 15):
        diag = p_ref[0, c - 1:c - 1 + n] + p_ref[0, c + 1:c + 1 + n] + p_ref[1, c:c + n]
        inv = jnp.where(s_ext[c:c + n] > 0, 1.0 / diag, 0.0)
        inv_ref[c:c + n] = inv
        q_ref[5, c:c + n] = diag
    arrived(1)
    for c, n in chunks(1, 15):
        for i in range(3):
            v_ref[i, c:c + n] = r_ext[i, c:c + n] * inv_ref[c:c + n]

    for sweep in range(SWEEPS):
        lo, hi = 2 + sweep, 14 - sweep
        for c, n in chunks(lo - 1, hi + 1):
            s = s_ext[c:c + n]
            ux, uy, uz = [s * v_ref[i, c:c + n] for i in range(3)]
            yp, ym = yshift(ux, 1), yshift(ux, -1)
            a = 2.0 * ux + (yp + ym)
            q_ref[1, c:c + n] = yp - ym
            p_ref[0, c:c + n] = 0.5 * a + 0.25 * (zshift(a, 1) + zshift(a, -1))
            q_ref[2, c:c + n] = zshift(ux, 1) - zshift(ux, -1)
            yp, ym = yshift(uy, 1), yshift(uy, -1)
            a = 2.0 * uy + (yp + ym)
            dy_uy = yp - ym
            p_ref[1, c:c + n] = 0.5 * a + 0.25 * (zshift(a, 1) + zshift(a, -1))
            q_ref[4, c:c + n] = zshift(dy_uy, 1) - zshift(dy_uy, -1)
            zp, zm = zshift(uz, 1), zshift(uz, -1)
            a = 2.0 * uz + (zp + zm)
            dz_uz = zp - zm
            p_ref[2, c:c + n] = 0.5 * a + 0.25 * (yshift(a, 1) + yshift(a, -1))
            q_ref[3, c:c + n] = yshift(dz_uz, 1) - yshift(dz_uz, -1)
            q_ref[0, c:c + n] = dy_uy + dz_uz
        for c, n in chunks(lo, hi):
            mid, up, down = slice(c, c + n), slice(c + 1, c + 1 + n), slice(c - 1, c - 1 + n)
            s = s_ext[mid]
            inv = inv_ref[mid]
            factor = q_ref[5, mid] + 2.0 * s
            cross = [
                q_ref[0, up] - q_ref[0, down],
                q_ref[1, up] - q_ref[1, down] + q_ref[3, mid],
                q_ref[2, up] - q_ref[2, down] + q_ref[4, mid],
            ]
            for i in range(3):
                v = v_ref[i, mid]
                smooth = p_ref[i, up] + p_ref[i, down] + 2.0 * p_ref[i, mid]
                av = factor * v - smooth - 0.25 * cross[i]
                new = v + (r_ext[i, mid] - av) * inv
                if sweep < SWEEPS - 1:
                    v_ref[i, mid] = new
                else:
                    adj_out[i, c - 4:c - 4 + n] = new[:, 0:8]

    rows = adj_out.shape[1] * adj_out.shape[2]
    flat = adj_out[...].reshape(3 * rows, 128)
    top = flat.astype(jnp.bfloat16)
    rest = (flat - top.astype(jnp.float32)).astype(jnp.bfloat16)
    at = jnp.dot(top, zhot[...], preferred_element_type=jnp.float32)
    at = at + jnp.dot(rest, zhot[...], preferred_element_type=jnp.float32)
    row_mask = lax.broadcasted_iota(jnp.int32, (rows, slots), 0) == row_of
    live_f = live_v[...].astype(jnp.float32)
    sens = []
    for i in range(3):
        picked = jnp.where(row_mask, at[i * rows:(i + 1) * rows], 0.0)
        adj_at = jnp.sum(picked, axis=0, keepdims=True)
        sens.append(live_f * (direct_v[i] - metric_v[i] * adj_at))
    total = jnp.zeros((48, lows), jnp.float32)
    for e in range(8):
        parts = jnp.concatenate([mw[e] * sens[i] for i in range(3)], axis=0)
        top = parts.astype(jnp.bfloat16).astype(jnp.float32)
        both = jnp.concatenate([top, parts - top], axis=0).astype(jnp.bfloat16)
        total = total + lax.dot_general(
            both, lohot[e], (((1,), (1,)), ((), ())), preferred_element_type=jnp.float32
        )
    total = total[0:24] + total[24:48]
    for h in range(6):
        for i in range(3):
            send_g[h, i:i + 1] = total[8 * i + h:8 * i + h + 1]

    sends = {
        h: pltpu.make_async_remote_copy(
            send_g.at[h], recv_g.at[h], g_send.at[h], g_recv.at[h],
            device_id=owner(h), device_id_type=MESH)
        for h in (3, 5, 4, 0, 2)
    }
    for copy in sends.values():
        copy.start()
    for k, (dx, dy) in enumerate(DIRS):
        @pl.when(exists(dx, dy))
        def _(k=k):
            for copy in halo(k):
                copy.wait_send()
    acc = send_g[1, 0:3]
    for h, copy in sends.items():
        copy.wait_recv()
        acc = acc + recv_g[h, 0:3]
    grad_out[...] = acc
    for copy in sends.values():
        copy.wait_send()


def write(adj, grad, adj_hbm, grad_hbm, sem):
    copies = [
        pltpu.make_async_copy(adj, adj_hbm, sem.at[0]),
        pltpu.make_async_copy(grad, grad_hbm, sem.at[1]),
    ]
    for copy in copies:
        copy.start()
    for copy in copies:
        copy.wait()


def local(stiffness, adjoint_rhs, surf_cell, surf_live, ffd_index, ffd_weight, surf_direct, surf_metric):
    n_axial, n_span = lax.axis_size("axial"), lax.axis_size("span")
    owned = NFFD // (n_axial * n_span)
    lows = max(owned, 128)
    slots = surf_cell.shape[1]
    f32, i32 = jnp.float32, jnp.int32
    any_spec = pl.BlockSpec(memory_space=pl.ANY)
    dma = pltpu.SemaphoreType.DMA
    adjoint, grad = pl.pallas_call(
        functools.partial(kernel, n_axial, n_span),
        out_shape=(
            pltpu.VMEM(adjoint_rhs.shape, f32),
            pltpu.VMEM((3, lows), f32),
        ),
        in_specs=[any_spec] * 8,
        out_specs=(pl.BlockSpec(memory_space=pltpu.VMEM),) * 2,
        scratch_shapes=[
            pltpu.VMEM((16, 16, 128), f32),
            pltpu.VMEM((3, 16, 16, 128), f32),
            pltpu.VMEM((16, 16, 128), f32),
            pltpu.VMEM((3, 16, 16, 128), f32),
            pltpu.VMEM((3, 16, 16, 128), f32),
            pltpu.VMEM((6, 16, 16, 128), f32),
            pltpu.VMEM(surf_cell.shape, i32),
            pltpu.VMEM(surf_live.shape, i32),
            pltpu.VMEM(ffd_index.shape, i32),
            pltpu.VMEM(ffd_weight.shape, f32),
            pltpu.VMEM(surf_direct.shape, f32),
            pltpu.VMEM(surf_metric.shape, f32),
            pltpu.VMEM((128, slots), jnp.bfloat16),
            pltpu.VMEM((8, lows, slots), jnp.bfloat16),
            pltpu.VMEM((8, 8, slots), f32),
            pltpu.VMEM((6, 8, lows), f32),
            pltpu.VMEM((6, 8, lows), f32),
            dma((8, 2)),
            dma((8, 2)),
            dma((6,)),
            dma((6,)),
            dma((8,)),
        ],
        compiler_params=pltpu.CompilerParams(collective_id=0, has_side_effects=True),
    )(stiffness, adjoint_rhs, surf_cell, surf_live, ffd_index, ffd_weight, surf_direct, surf_metric)
    vmem_spec = pl.BlockSpec(memory_space=pltpu.VMEM)
    adjoint, grad = pl.pallas_call(
        write,
        out_shape=(
            jax.ShapeDtypeStruct(adjoint_rhs.shape, f32),
            jax.ShapeDtypeStruct((3, lows), f32),
        ),
        in_specs=[vmem_spec] * 2,
        out_specs=(any_spec, any_spec),
        scratch_shapes=[dma((2,))],
    )(*(pltpu.with_memory_space_constraint(a, pltpu.VMEM) for a in (adjoint, grad)))
    return adjoint, grad[:, :owned].T


def solution(mesh):
    return jax.shard_map(
        local,
        mesh=mesh,
        in_specs=(
            P("axial", "span", None),
            P(None, "axial", "span", None),
            P("axial", "span"),
            P("axial", "span"),
            P(None, "axial", "span"),
            P(None, "axial", "span"),
            P(None, "axial", "span"),
            P(None, "axial", "span"),
        ),
        out_specs=(P(None, "axial", "span", None), P(("axial", "span"), None)),
        check_vma=False,
    )
```
